256 devices in a mesh: seq: 64 (over x, z_hi, y), tp: 4 (over z_lo, core).
Axes of the slice: x: 4, y: 4, z: 8 (z_hi: 4, z_lo: 2; z = z_hi * 2 + z_lo), core: 2. Of those that a mesh axis runs over, the one named last changes fastest.
Arguments:
- queries: bfloat16 [16384, 4096], P('seq', 'tp'), may hold values from -4.5 to 4.5
- sequence_keys: bfloat16 [16384, 1024], P('seq', 'tp'), may hold values from -4.5 to 4.5
- sequence_values: bfloat16 [16384, 1024], P('seq', 'tp'), may hold values from -6 to 6
- output_gradient: bfloat16 [16384, 4096], P('seq', 'tp'), may hold values from -6 to 6
- enc_keys: bfloat16 [4096, 16, 1024], P('seq', 'tp'), may hold values from -4.5 to 4.5
- encoded_values: bfloat16 [4096, 16, 1024], P('seq', 'tp'), may hold values from -6 to 6
- nbr_owner: int32 [256, 4], P('seq'), may hold values from 0 to 63, as said below
- nbr_slot: int32 [256, 4], P('seq'), may hold values from 0 to 63
Outputs:
- attended: bfloat16 [16384, 4096], P('seq', 'tp')
- query_gradient: bfloat16 [16384, 4096], P('seq', 'tp')
- key_gradient: bfloat16 [16384, 1024], P('seq', 'tp')
- value_gradient: bfloat16 [16384, 1024], P('seq', 'tp')
- encoded_key_gradient: bfloat16 [4096, 16, 1024], P('seq', 'tp')
- encoded_value_gradient: bfloat16 [4096, 16, 1024], P('seq', 'tp')
The draws below stay inside these ranges and needn't reach their ends.
Inputs may be any that keep to these rules, and one draw needn't show every extreme that they name: `nbr_owner`: among the 16 entries of the stretches of one index of seq, at most 2 name the same owner; in every draw one owner is named exactly 2 times by the entries of every index of seq. The same owner may appear twice in one stretch.
All inputs are finite; a program needn't handle non-finite values.
Results may differ from the reference program's by a relative error of at most 0.0083.
Values may be sent and summed in bfloat16 or wider, within the bound.
A program may use at most 64 MiB of HBM per device.

```python
import math
import jax
import jax.numpy as jnp
from jax import lax

QUERY_HEADS = 32
KEY_VALUE_HEADS = 8
HEAD_SIZE = 128
TOK_DEV = 256
SPAN_TOKENS = 64
NEIGHBOUR_COUNT = 4
NEIGHBOUR_LENGTH = 16
ENC_DEV = 64
WINDOW_KEYS = 128
LOCAL_SPANS = 4
CAP = 2
SEQUENCE_TOKENS = 16384
SPAN_COUNT = 256
ENCODED_SLOTS = 4096
N_SEQ = 64


def base_region(key, salt, shape):
    return jnp.clip(jax.random.normal(jax.random.fold_in(key, salt), shape, jnp.float32), -4.5, 4.5)


def draw_queries(key, part):
    region = base_region(key, 11, (SEQUENCE_TOKENS, QUERY_HEADS * HEAD_SIZE))
    return region.astype(jnp.bfloat16)


def draw_sequence_keys(key, part):
    region = base_region(key, 12, (SEQUENCE_TOKENS, KEY_VALUE_HEADS * HEAD_SIZE))
    return region.astype(jnp.bfloat16)


def draw_enc_keys(key, part):
    region = base_region(key, 13, (ENCODED_SLOTS, NEIGHBOUR_LENGTH, KEY_VALUE_HEADS * HEAD_SIZE))
    return region.astype(jnp.bfloat16)


def draw_nbr_owner(key, part):
    requests = LOCAL_SPANS * NEIGHBOUR_COUNT
    extra_rows = requests - CAP
    spread = min(N_SEQ - 1, max(-(-extra_rows // CAP), 2 * extra_rows // 3))
    hot_owner = jax.random.randint(jax.random.fold_in(key, 21), (), 0, N_SEQ).astype(jnp.int32)

    def one_device(device_key):
        shuffled = jax.random.permutation(jax.random.fold_in(device_key, 1), N_SEQ - 1).astype(jnp.int32)
        others = (hot_owner + 1 + shuffled) % N_SEQ
        listed = jnp.concatenate([jnp.full((CAP,), hot_owner, jnp.int32), others[jnp.arange(extra_rows, dtype=jnp.int32) % spread]])
        return listed[jax.random.permutation(jax.random.fold_in(device_key, 2), requests)]
    device_keys = jax.random.split(jax.random.fold_in(key, 22), N_SEQ)
    return jax.vmap(one_device)(device_keys).reshape(SPAN_COUNT, NEIGHBOUR_COUNT).astype(jnp.int32)


def touch_ends(array, own_key, least, largest):
    extent = array.shape
    index_at = [jax.random.randint(jax.random.fold_in(own_key, axis), (), 0, extent[axis]) for axis in range(len(extent))]
    array = array.at[tuple(index_at)].set(least)
    longest = extent.index(max(extent))
    index_at[longest] = (index_at[longest] + 1) % extent[longest]
    return array.at[tuple(index_at)].set(largest)


def block_levels(own_key, shape, cuts, smallest, largest):
    factor_of, own = 1.0, jax.random.fold_in(own_key, 6)
    for axis_at, blocks in cuts:
        draws = jnp.exp(jax.random.uniform(jax.random.fold_in(own, axis_at), (blocks,), jnp.float32, smallest / len(cuts), largest / len(cuts)))
        factor_of = factor_of * jnp.repeat(draws, shape[axis_at] // blocks).reshape([-1 if axis == axis_at else 1 for axis in range(len(shape))])
    return factor_of


def bell_draw(own_key, dims, scale, most, shards=(), kind=jnp.bfloat16):
    loudness = block_levels(own_key, dims, shards, -0.22, 0.18) if shards else 1.0
    array = jax.random.normal(own_key, dims, jnp.float32) * scale * loudness
    return jnp.minimum(jnp.maximum(array, -most), most).astype(kind)


def setup_inputs(seed: int = 0) -> dict:
    splits = jax.random.split(jax.random.key(seed), 9)
    return {
        "queries": draw_queries(jax.random.fold_in(splits[8], 71), 0),
        "sequence_keys": draw_sequence_keys(jax.random.fold_in(splits[8], 71), 0),
        "sequence_values": bell_draw(splits[2], (SEQUENCE_TOKENS, KEY_VALUE_HEADS * HEAD_SIZE), 1.0, 6.0, ((0, 64), (1, 4))),
        "output_gradient": bell_draw(splits[3], (SEQUENCE_TOKENS, QUERY_HEADS * HEAD_SIZE), 1.0, 6.0, ((0, 64), (1, 4))),
        "enc_keys": draw_enc_keys(jax.random.fold_in(splits[8], 71), 0),
        "encoded_values": bell_draw(splits[5], (ENCODED_SLOTS, NEIGHBOUR_LENGTH, KEY_VALUE_HEADS * HEAD_SIZE), 1.0, 6.0, ((0, 64), (1, 4))),
        "nbr_owner": draw_nbr_owner(jax.random.fold_in(splits[8], 71), 0),
        "nbr_slot": touch_ends(jax.random.randint(splits[7], (SPAN_COUNT, NEIGHBOUR_COUNT), 0, ENC_DEV), jax.random.fold_in(splits[7], 1), 0, ENC_DEV - 1).astype(jnp.int32),
    }


HIGHEST = lax.Precision.HIGHEST

def settle(array_f):
    return lax.optimization_barrier(array_f.astype(jnp.bfloat16)).astype(jnp.float32)

def attend(query_in, rows_of_keys, rows_of_values, grad_rows, allowed):
    score_scale = 1.0 / math.sqrt(HEAD_SIZE)
    scores = jnp.einsum('cqhgd,ckhd->chgqk', query_in, rows_of_keys, precision=HIGHEST) * score_scale
    if allowed is not None:
        scores = jnp.where(allowed, scores, -jnp.inf)
    top_score = lax.optimization_barrier(jnp.max(scores, axis=-1, keepdims=True))
    raised = jnp.exp(scores - top_score)
    probability = raised / lax.optimization_barrier(jnp.sum(raised, axis=-1, keepdims=True))
    weights = settle(probability)
    attended = jnp.einsum('chgqk,ckhd->cqhgd', weights, rows_of_values, precision=HIGHEST)
    grad_prob = jnp.einsum('cqhgd,ckhd->chgqk', grad_rows, rows_of_values, precision=HIGHEST)
    delta_row = lax.optimization_barrier(jnp.sum(probability * grad_prob, axis=-1, keepdims=True))
    grad_score = settle(probability * (grad_prob - delta_row) * score_scale)
    query_gradient = jnp.einsum('chgqk,ckhd->cqhgd', grad_score, rows_of_keys, precision=HIGHEST)
    key_gradient = jnp.einsum('chgqk,cqhgd->ckhd', grad_score, query_in, precision=HIGHEST)
    value_gradient = jnp.einsum('chgqk,cqhgd->ckhd', weights, grad_rows, precision=HIGHEST)
    return (attended, query_gradient, key_gradient, value_gradient)

def self_part(queries, sequence_keys, sequence_values, output_gradient):
    heads_per_group = QUERY_HEADS // KEY_VALUE_HEADS
    rows_per_block = min(512, TOK_DEV)
    key_span = WINDOW_KEYS + rows_per_block
    count_blocks = SEQUENCE_TOKENS // rows_per_block
    query_total = queries.astype(jnp.float32).reshape(count_blocks, rows_per_block, KEY_VALUE_HEADS, heads_per_group, HEAD_SIZE)
    gradient_total = output_gradient.astype(jnp.float32).reshape(count_blocks, rows_per_block, KEY_VALUE_HEADS, heads_per_group, HEAD_SIZE)
    padding_rows = jnp.zeros((WINDOW_KEYS, KEY_VALUE_HEADS, HEAD_SIZE), jnp.float32)
    key_padded_rows = jnp.concatenate([padding_rows, sequence_keys.astype(jnp.float32).reshape(SEQUENCE_TOKENS, KEY_VALUE_HEADS, HEAD_SIZE)], 0)
    value_padded_rows = jnp.concatenate([padding_rows, sequence_values.astype(jnp.float32).reshape(SEQUENCE_TOKENS, KEY_VALUE_HEADS, HEAD_SIZE)], 0)

    def block_step(carried, sliced):
        key_accumulator, value_accumulator = carried
        number, query_block, grad_block = sliced
        first_row = number * rows_per_block
        key_block = lax.dynamic_slice_in_dim(key_padded_rows, first_row, key_span, 0)
        value_block = lax.dynamic_slice_in_dim(value_padded_rows, first_row, key_span, 0)
        rows_at = first_row + jnp.arange(rows_per_block, dtype=jnp.int32)[:, None]
        cols_at = first_row - WINDOW_KEYS + jnp.arange(key_span, dtype=jnp.int32)[None, :]
        allowed = (cols_at >= 0) & (cols_at <= rows_at) & (cols_at > rows_at - WINDOW_KEYS)
        attended, query_gradient, key_gradient, value_gradient = attend(query_block[None], key_block[None], value_block[None], grad_block[None], allowed[None, None, None])
        key_accumulator = lax.dynamic_update_slice_in_dim(key_accumulator, lax.dynamic_slice_in_dim(key_accumulator, first_row, key_span, 0) + key_gradient[0], first_row, 0)
        value_accumulator = lax.dynamic_update_slice_in_dim(value_accumulator, lax.dynamic_slice_in_dim(value_accumulator, first_row, key_span, 0) + value_gradient[0], first_row, 0)
        return ((key_accumulator, value_accumulator), (attended[0], query_gradient[0]))
    empty_accumulator = jnp.zeros((WINDOW_KEYS + SEQUENCE_TOKENS, KEY_VALUE_HEADS, HEAD_SIZE), jnp.float32)
    (key_accumulator, value_accumulator), (attended, query_gradient) = lax.scan(block_step, (empty_accumulator, empty_accumulator), (jnp.arange(count_blocks, dtype=jnp.int32), query_total, gradient_total))
    return (attended.reshape(SEQUENCE_TOKENS, QUERY_HEADS * HEAD_SIZE), query_gradient.reshape(SEQUENCE_TOKENS, QUERY_HEADS * HEAD_SIZE), key_accumulator[WINDOW_KEYS:].reshape(SEQUENCE_TOKENS, KEY_VALUE_HEADS * HEAD_SIZE), value_accumulator[WINDOW_KEYS:].reshape(SEQUENCE_TOKENS, KEY_VALUE_HEADS * HEAD_SIZE))

def cross_part(queries, output_gradient, enc_keys, encoded_values, nbr_owner, nbr_slot):
    heads_per_group = QUERY_HEADS // KEY_VALUE_HEADS
    query_total = queries.astype(jnp.float32).reshape(N_SEQ, LOCAL_SPANS, SPAN_TOKENS, KEY_VALUE_HEADS, heads_per_group, HEAD_SIZE)
    gradient_total = output_gradient.astype(jnp.float32).reshape(N_SEQ, LOCAL_SPANS, SPAN_TOKENS, KEY_VALUE_HEADS, heads_per_group, HEAD_SIZE)
    slot_all = (nbr_owner * ENC_DEV + nbr_slot).astype(jnp.int32)
    slot_groups = slot_all.reshape(N_SEQ, LOCAL_SPANS * NEIGHBOUR_COUNT)
    stored_key_rows = enc_keys.astype(jnp.float32)
    stored_value_rows = encoded_values.astype(jnp.float32)

    def one_group(sliced):
        query_in, grad_in, slot_indices = sliced
        rows_of_keys = jnp.take(stored_key_rows, slot_indices, axis=0).reshape(LOCAL_SPANS, NEIGHBOUR_COUNT * NEIGHBOUR_LENGTH, KEY_VALUE_HEADS, HEAD_SIZE)
        rows_of_values = jnp.take(stored_value_rows, slot_indices, axis=0).reshape(LOCAL_SPANS, NEIGHBOUR_COUNT * NEIGHBOUR_LENGTH, KEY_VALUE_HEADS, HEAD_SIZE)
        attended, query_gradient, key_gradient, value_gradient = attend(query_in, rows_of_keys, rows_of_values, grad_in, None)
        return (attended, query_gradient, key_gradient.reshape(LOCAL_SPANS * NEIGHBOUR_COUNT, NEIGHBOUR_LENGTH, KEY_VALUE_HEADS * HEAD_SIZE), value_gradient.reshape(LOCAL_SPANS * NEIGHBOUR_COUNT, NEIGHBOUR_LENGTH, KEY_VALUE_HEADS * HEAD_SIZE))
    result_list = lax.map(one_group, (query_total, gradient_total, slot_groups))
    flattened_slots = slot_all.reshape(SPAN_COUNT * NEIGHBOUR_COUNT)
    encoded_key_gradient = jax.ops.segment_sum(result_list[2].reshape(SPAN_COUNT * NEIGHBOUR_COUNT, NEIGHBOUR_LENGTH, KEY_VALUE_HEADS * HEAD_SIZE), flattened_slots, num_segments=ENCODED_SLOTS)
    encoded_value_gradient = jax.ops.segment_sum(result_list[3].reshape(SPAN_COUNT * NEIGHBOUR_COUNT, NEIGHBOUR_LENGTH, KEY_VALUE_HEADS * HEAD_SIZE), flattened_slots, num_segments=ENCODED_SLOTS)
    return (result_list[0].reshape(SEQUENCE_TOKENS, QUERY_HEADS * HEAD_SIZE), result_list[1].reshape(SEQUENCE_TOKENS, QUERY_HEADS * HEAD_SIZE), encoded_key_gradient, encoded_value_gradient)

def reference(queries, sequence_keys, sequence_values, output_gradient, enc_keys, encoded_values, nbr_owner, nbr_slot):
    self_out, self_qgrad, key_gradient, value_gradient = self_part(queries, sequence_keys, sequence_values, output_gradient)
    cross_out, cross_qgrad, encoded_key_gradient, encoded_value_gradient = cross_part(queries, output_gradient, enc_keys, encoded_values, nbr_owner, nbr_slot)
    attended = (self_out + cross_out).astype(jnp.bfloat16)
    query_gradient = (self_qgrad + cross_qgrad).astype(jnp.bfloat16)
    return (attended, query_gradient, key_gradient.astype(jnp.bfloat16), value_gradient.astype(jnp.bfloat16), encoded_key_gradient.astype(jnp.bfloat16), encoded_value_gradient.astype(jnp.bfloat16))
```

```python
import math

import jax
import jax.numpy as jnp
from jax import lax
from jax.experimental import pallas as pl
from jax.experimental.pallas import tpu as pltpu
from jax.sharding import PartitionSpec as P

HEAD = 128
GROUP = 4
SCALE = 1.0 / math.sqrt(HEAD)
NEG = -1e30
MESH = pl.DeviceIdType.MESH
BF = jnp.bfloat16
F32 = jnp.float32
I32 = jnp.int32


def dot_nn(a, b):
    return lax.dot_general(a, b, (((1,), (0,)), ((), ())), preferred_element_type=F32)


def dot_nt(a, b):
    return lax.dot_general(a, b, (((1,), (1,)), ((), ())), preferred_element_type=F32)


def dot_tn(a, b):
    return lax.dot_general(a, b, (((0,), (0,)), ((), ())), preferred_element_type=F32)


def attend(q, k, v, g, allowed):
    s = jnp.where(allowed, dot_nt(q, k) * SCALE, NEG)
    e = jnp.exp(s - jnp.max(s, axis=-1, keepdims=True))
    p = e * (1.0 / jnp.sum(e, axis=-1, keepdims=True))
    w = p.astype(BF)
    out = dot_nn(w, v)
    dp = dot_nt(g, v)
    delta = jnp.sum(p * dp, axis=-1, keepdims=True)
    ds = (p * (dp - delta) * SCALE).astype(BF)
    return out, dot_nn(ds, k), dot_tn(ds, q), dot_tn(w, g)


def kernel(
    own_ref, slot_ref, q, g, k, v, ek, ev,
    att, qg, kg, vg, ekg, evg,
    send_a, recv_a, send_b, recv_b, tab_a, tab_b, g1, g2, g3, g4,
    halo, back_send, back_recv, kacc, vacc, oacc, qacc, kmat, vmat, sel,
    send1, recv1, send2, recv2, send3, recv3, send4, recv4,
    sem_i, sem_h, s1, r1, s2, r2, s3, r3, s4, r4,
):
    me = lax.axis_index("seq")
    t = lax.axis_index("tp")
    x = lax.div(me, 16)
    z = lax.rem(lax.div(me, 4), 4)
    y = lax.rem(me, 4)

    def device(dx, dz, dy, dt):
        return (
            lax.rem(x + dx, 4) * 16 + lax.rem(z + dz, 4) * 4 + lax.rem(y + dy, 4),
            lax.rem(t + dt, 4),
        )

    def seq_peer(d):
        return device(lax.div(d, 16), lax.rem(lax.div(d, 4), 4), lax.rem(d, 4), 0)

    barrier = pltpu.get_barrier_semaphore()

    def greet(d, c):
        pl.semaphore_signal(barrier, 1, device_id=seq_peer(d), device_id_type=MESH)
        return c

    lax.fori_loop(1, 64, greet, 0)
    for dz in range(4):
        for dt in range(1, 4):
            pl.semaphore_signal(barrier, 1, device_id=device(0, dz, 0, dt), device_id_type=MESH)

    lane = lax.broadcasted_iota(I32, (1, 128), 1)
    owners = [own_ref[i // 4, i % 4] for i in range(16)]
    slots = [slot_ref[i // 4, i % 4] for i in range(16)]
    row_a = jnp.full((1, 128), -1, I32)
    row_b = jnp.zeros((1, 128), I32)
    row_c = jnp.zeros((1, 128), I32)
    for i in range(16):
        rank = jnp.int32(0)
        for j in range(i):
            rank = rank + (owners[j] == owners[i]).astype(I32)
        place = owners[i] * 2 + rank
        row_a = jnp.where(lane == place, slots[i], row_a)
        row_b = jnp.where(lane == place, i, row_b)
        row_c = jnp.where(lane == i, place, row_c)
        zo = lax.rem(lax.div(owners[i], 4), 4)
        g3[i] = lax.rem(z - zo + 4, 4) * 16 + i
    send_a[0] = row_a
    recv_a[0] = row_a
    rows_bc = jnp.concatenate([row_b, row_c], 0)
    send_b[0] = rows_bc
    recv_b[0] = rows_bc

    pl.semaphore_wait(barrier, 75)

    nxt = (lax.rem(me + 1, 64), t)
    prv = (lax.rem(me + 63, 64), t)

    def remote(src, dst, ssem, rsem, dev):
        return pltpu.make_async_remote_copy(
            src_ref=src, dst_ref=dst, send_sem=ssem, recv_sem=rsem,
            device_id=dev, device_id_type=MESH,
        )

    def await_bytes(ref, sem):
        pltpu.make_async_copy(ref, ref, sem).wait()

    def tell(d, c):
        remote(send_a.at[0], recv_a.at[d], sem_i.at[0], sem_i.at[1], seq_peer(d)).start()
        return c

    lax.fori_loop(1, 64, tell, 0)
    for dz in range(1, 4):
        remote(send_b.at[0], recv_b.at[dz], sem_i.at[2], sem_i.at[3], device(0, dz, 0, 0)).start()
    halo_k = remote(k.at[pl.ds(128, 128)], halo.at[0], sem_h.at[0], sem_h.at[1], nxt)
    halo_v = remote(v.at[pl.ds(128, 128)], halo.at[1], sem_h.at[2], sem_h.at[3], nxt)
    halo_k.start()
    halo_v.start()

    def self_block(b, hh):
        cols = pl.ds(pl.multiple_of(hh * 128, 128), 128)
        rows = pl.ds(128 * b, 128)
        if b == 0:
            kk = jnp.concatenate([halo[0, :, cols], k[0:128, cols]], 0)
            vv = jnp.concatenate([halo[1, :, cols], v[0:128, cols]], 0)
        else:
            kk, vv = k[:, cols], v[:, cols]
        heads = [pl.ds(pl.multiple_of(hh * 512 + 128 * u, 128), 128) for u in range(4)]
        qq = jnp.concatenate([q[rows, h] for h in heads], 0)
        gg = jnp.concatenate([g[rows, h] for h in heads], 0)
        r = lax.rem(lax.broadcasted_iota(I32, (512, 256), 0), 128)
        c = lax.broadcasted_iota(I32, (512, 256), 1)
        allowed = (c > r) & (c <= r + 128)
        if b == 0:
            allowed = allowed & (c >= jnp.where(me > 0, 0, 128))
        out, dq, dk, dv = attend(qq, kk, vv, gg, allowed)
        for u in range(4):
            oacc[rows, heads[u]] = out[128 * u : 128 * u + 128]
            qacc[rows, heads[u]] = dq[128 * u : 128 * u + 128]
        if b == 0:
            kacc[0:256, cols] = dk
            vacc[0:256, cols] = dv
            back_send[0, :, cols] = dk[0:128].astype(BF)
            back_send[1, :, cols] = dv[0:128].astype(BF)
        else:
            kacc[128:256, cols] = kacc[128:256, cols] + dk[0:128]
            vacc[128:256, cols] = vacc[128:256, cols] + dv[0:128]
            kacc[256:384, cols] = dk[128:256]
            vacc[256:384, cols] = dv[128:256]

    halo_k.wait()
    halo_v.wait()

    def self0(hh, c):
        self_block(0, hh)
        return c

    lax.fori_loop(0, 2, self0, 0)
    back_k = remote(back_send.at[0], back_recv.at[0], sem_h.at[4], sem_h.at[5], prv)
    back_v = remote(back_send.at[1], back_recv.at[1], sem_h.at[6], sem_h.at[7], prv)
    back_k.start()
    back_v.start()

    await_bytes(recv_a.at[pl.ds(1, 63)], sem_i.at[1])
    await_bytes(recv_b.at[pl.ds(1, 3)], sem_i.at[3])
    copy_a = pltpu.make_async_copy(recv_a, tab_a, sem_i.at[4])
    copy_b = pltpu.make_async_copy(recv_b, tab_b, sem_i.at[5])
    copy_a.start()
    copy_b.start()
    copy_a.wait()
    copy_b.wait()

    def fill1(d, c):
        dx, dy = lax.div(d, 4), lax.rem(d, 4)
        for dz in range(4):
            src = lax.rem(4 - dx, 4) * 16 + ((4 - dz) % 4) * 4 + lax.rem(4 - dy, 4)
            for rank in range(2):
                g1[d * 8 + dz * 2 + rank] = jnp.maximum(tab_a[src, 0, 2 * me + rank], 0)
        return c

    lax.fori_loop(0, 16, fill1, 0)

    def plane_peer(d):
        return device(lax.div(d, 4), 0, lax.rem(d, 4), 0)

    for kv in range(2):
        store = (ek, ev)[kv]
        for dt in range(4):
            c = kv * 4 + dt
            tt = lax.rem(t + dt, 4)
            for m in range(8):
                recv1[c][m] = store[g1[m], tt]

            def gather1(d, carry, c=c, tt=tt, store=store):
                for m in range(8):
                    send1[c][d * 8 + m] = store[g1[d * 8 + m], tt]
                return carry

            lax.fori_loop(1, 16, gather1, 0)

            def start1(d, carry, c=c):
                part = pl.ds(d * 8, 8)
                remote(send1[c].at[part], recv1[c].at[part], s1.at[c], r1.at[c], plane_peer(d)).start()
                return carry

            lax.fori_loop(1, 16, start1, 0)

    def fill2(i, c):
        for dz in range(4):
            place = tab_b[(4 - dz) % 4, 1, i]
            owner, rank = lax.div(place, 2), lax.rem(place, 2)
            ox, oy = lax.div(owner, 16), lax.rem(owner, 4)
            dx, dy = lax.rem(x - ox + 4, 4), lax.rem(y - oy + 4, 4)
            g2[dz * 16 + i] = (dx * 4 + dy) * 8 + dz * 2 + rank
        return c

    lax.fori_loop(0, 16, fill2, 0)

    def fill4(d, c):
        dx, dy = lax.div(d, 4), lax.rem(d, 4)
        owner = lax.rem(x + dx, 4) * 16 + z * 4 + lax.rem(y + dy, 4)
        for dz in range(4):
            for rank in range(2):
                g4[d * 8 + dz * 2 + rank] = dz * 16 + tab_b[dz, 0, owner * 2 + rank]
        return c

    lax.fori_loop(0, 16, fill4, 0)

    row_at = lax.broadcasted_iota(I32, (512, 128), 0)
    for w in range(8):
        want = jnp.full((1, 128), -1, I32)
        for n in range(16):
            p = w * 16 + n
            d, dz, rank = p // 8, (p // 2) % 4, p % 2
            got = tab_a[(d // 4) * 16 + dz * 4 + d % 4, 0, 2 * me + rank]
            want = jnp.where(lax.div(lane, 8) == n, got * 8 + lax.rem(lane, 8), want)
        sel[:, pl.ds(128 * w, 128)] = jnp.where(row_at == want, 1.0, 0.0).astype(BF)

    def self1(hh, c):
        self_block(1, hh)
        return c

    lax.fori_loop(0, 2, self1, 0)

    for kv in range(2):
        for dt in range(4):
            c = kv * 4 + dt
            await_bytes(recv1[c].at[pl.ds(8, 120)], r1.at[c])
            if dt == 0:
                for i in range(16):
                    recv2[kv][i] = recv1[c][g2[i]]

            def gather2(dz, carry, c=c):
                for i in range(16):
                    send2[c][dz * 16 + i] = recv1[c][g2[dz * 16 + i]]
                return carry

            lax.fori_loop(1 if dt == 0 else 0, 4, gather2, 0)
            for dz in range(1 if dt == 0 else 0, 4):
                remote(
                    send2[c].at[pl.ds(dz * 16, 16)],
                    recv2[kv].at[pl.ds(dt * 64 + dz * 16, 16)],
                    s2.at[c], r2.at[c], device(0, dz, 0, dt),
                ).start()

    for kv in range(2):
        for dt in range(4):
            low = 16 if dt == 0 else 0
            await_bytes(recv2[kv].at[pl.ds(dt * 64 + low, 64 - low)], r2.at[kv * 4 + dt])
        mat = (kmat, vmat)[kv]
        for i in range(16):
            for dt in range(4):
                mat[pl.ds(i * 32 + dt * 8, 8), :] = recv2[kv][g3[i] + dt * 64]

    def cross(cc, carry):
        rows = pl.ds(pl.multiple_of(cc * 64, 64), 64)
        near = pl.ds(pl.multiple_of(cc * 128, 128), 128)
        qq = jnp.concatenate([q[rows, 128 * h : 128 * h + 128] for h in range(8)], 0)
        gg = jnp.concatenate([g[rows, 128 * h : 128 * h + 128] for h in range(8)], 0)
        r = lax.broadcasted_iota(I32, (512, 128), 0)
        n = lax.broadcasted_iota(I32, (512, 128), 1)
        allowed = lax.div(r, 256) == lax.div(lax.rem(n, 8), 4)
        out, dq, dk, dv = attend(qq, kmat[near, :], vmat[near, :], gg, allowed)
        for h in range(8):
            cols = pl.ds(128 * h, 128)
            att[rows, cols] = (oacc[rows, cols] + out[64 * h : 64 * h + 64]).astype(BF)
            qg[rows, cols] = (qacc[rows, cols] + dq[64 * h : 64 * h + 64]).astype(BF)
        for kv in range(2):
            tiles = (dk, dv)[kv].astype(BF).reshape(16, 8, 128)
            for j in range(4):
                for dt in range(4):
                    send3[kv][dt * 16 + cc * 4 + j] = tiles[j * 4 + dt]
                recv3[kv * 4][cc * 4 + j] = tiles[j * 4]
        return carry

    lax.fori_loop(0, 4, cross, 0)

    for kv in range(2):
        for dt in range(4):
            c = kv * 4 + dt
            for dz in range(1 if dt == 0 else 0, 4):
                remote(
                    send3[kv].at[pl.ds(dt * 16, 16)],
                    recv3[c].at[pl.ds(dz * 16, 16)],
                    s3.at[c], r3.at[c], device(0, dz, 0, (4 - dt) % 4),
                ).start()

    for kv in range(2):
        for dt in range(4):
            c = kv * 4 + dt
            low = 16 if dt == 0 else 0
            await_bytes(recv3[c].at[pl.ds(low, 64 - low)], r3.at[c])
            for m in range(8):
                recv4[c][m] = recv3[c][g4[m]]

            def gather4(d, carry, c=c):
                for m in range(8):
                    send4[c][d * 8 + m] = recv3[c][g4[d * 8 + m]]
                return carry

            lax.fori_loop(1, 16, gather4, 0)

            def start4(d, carry, c=c):
                part = pl.ds(d * 8, 8)
                remote(send4[c].at[part], recv4[c].at[part], s4.at[c], r4.at[c], plane_peer(d)).start()
                return carry

            lax.fori_loop(1, 16, start4, 0)

    back_k.wait()
    back_v.wait()
    kg[0:128, :] = kacc[128:256, :].astype(BF)
    vg[0:128, :] = vacc[128:256, :].astype(BF)
    kg[128:256, :] = (kacc[256:384, :] + back_recv[0].astype(F32)).astype(BF)
    vg[128:256, :] = (vacc[256:384, :] + back_recv[1].astype(F32)).astype(BF)

    for kv in range(2):
        for dt in range(4):
            c = kv * 4 + dt
            await_bytes(recv4[c].at[pl.ds(8, 120)], r4.at[c])
            total = dot_nn(sel[...], recv4[c].reshape(1024, 128)[...])
            (ekg, evg)[kv][:, lax.rem(t + dt, 4)] = total.reshape(64, 8, 128).astype(BF)

    await_bytes(recv_a.at[pl.ds(1, 63)], sem_i.at[0])
    await_bytes(recv_b.at[pl.ds(1, 3)], sem_i.at[2])
    for c in range(8):
        low = 16 if c % 4 == 0 else 0
        await_bytes(send1[c].at[pl.ds(8, 120)], s1.at[c])
        await_bytes(send2[c].at[pl.ds(low, 64 - low)], s2.at[c])
        await_bytes(recv3[c].at[pl.ds(low, 64 - low)], s3.at[c])
        await_bytes(send4[c].at[pl.ds(8, 120)], s4.at[c])


def tiles(n):
    return pltpu.VMEM((n, 8, 128), BF)


def body(queries, seq_keys, seq_values, out_grad, enc_keys, enc_values, nbr_owner, nbr_slot):
    def to_tiles(e):
        return e.reshape(64, 4, 4, 2, 128).transpose(0, 2, 3, 1, 4).reshape(64, 4, 8, 128)

    def from_tiles(e):
        return e.reshape(64, 4, 2, 4, 128).transpose(0, 3, 1, 2, 4).reshape(64, 4, 1024)

    smem = pl.BlockSpec(memory_space=pltpu.SMEM)
    vmem = pl.BlockSpec(memory_space=pltpu.VMEM)
    dma = pltpu.SemaphoreType.DMA
    outs = pl.pallas_call(
        kernel,
        out_shape=(
            jax.ShapeDtypeStruct((256, 1024), BF),
            jax.ShapeDtypeStruct((256, 1024), BF),
            jax.ShapeDtypeStruct((256, 256), BF),
            jax.ShapeDtypeStruct((256, 256), BF),
            jax.ShapeDtypeStruct((64, 4, 8, 128), BF),
            jax.ShapeDtypeStruct((64, 4, 8, 128), BF),
        ),
        in_specs=[smem] * 2 + [vmem] * 6,
        out_specs=(vmem,) * 6,
        scratch_shapes=[
            pltpu.VMEM((1, 1, 128), I32),
            pltpu.VMEM((64, 1, 128), I32),
            pltpu.VMEM((1, 2, 128), I32),
            pltpu.VMEM((4, 2, 128), I32),
            pltpu.SMEM((64, 1, 128), I32),
            pltpu.SMEM((4, 2, 128), I32),
            pltpu.SMEM((128,), I32),
            pltpu.SMEM((64,), I32),
            pltpu.SMEM((16,), I32),
            pltpu.SMEM((128,), I32),
            pltpu.VMEM((2, 128, 256), BF),
            pltpu.VMEM((2, 128, 256), BF),
            pltpu.VMEM((2, 128, 256), BF),
            pltpu.VMEM((384, 256), F32),
            pltpu.VMEM((384, 256), F32),
            pltpu.VMEM((256, 1024), F32),
            pltpu.VMEM((256, 1024), F32),
            pltpu.VMEM((512, 128), BF),
            pltpu.VMEM((512, 128), BF),
            pltpu.VMEM((512, 1024), BF),
            [tiles(128)] * 8,
            [tiles(128)] * 8,
            [tiles(64)] * 8,
            [tiles(256)] * 2,
            [tiles(64)] * 2,
            [tiles(64)] * 8,
            [tiles(128)] * 8,
            [tiles(128)] * 8,
            dma((6,)),
            dma((8,)),
            dma((8,)),
            dma((8,)),
            dma((8,)),
            dma((8,)),
            dma((8,)),
            dma((8,)),
            dma((8,)),
            dma((8,)),
        ],
        compiler_params=pltpu.CompilerParams(
            collective_id=0, has_side_effects=True, vmem_limit_bytes=48 << 20
        ),
        name="retro",
    )(
        nbr_owner, nbr_slot, queries, out_grad, seq_keys, seq_values,
        to_tiles(enc_keys), to_tiles(enc_values),
    )
    att, qg, kg, vg, ekg, evg = outs
    return att, qg, kg, vg, from_tiles(ekg), from_tiles(evg)


def solution(mesh):
    shard = P("seq", "tp")
    store = P("seq", "tp", None)
    return jax.shard_map(
        body,
        mesh=mesh,
        in_specs=(shard, shard, shard, shard, store, store, P("seq", None), P("seq", None)),
        out_specs=(shard, shard, shard, shard, store, store),
        check_vma=False,
    )
```

```python
import math

import jax
import jax.numpy as jnp
from jax import lax
from jax.experimental import pallas as pl
from jax.experimental.pallas import tpu as pltpu
from jax.sharding import PartitionSpec as P

HEAD = 128
GROUP = 4
SCALE = 1.0 / math.sqrt(HEAD)
NEG = -1e30
AHEAD = 3
VMEM_MAIN = 48 << 20
LAG = 3
MESH = pl.DeviceIdType.MESH
BF = jnp.bfloat16
F32 = jnp.float32
I32 = jnp.int32


def dot_nn(a, b):
    return lax.dot_general(a, b, (((1,), (0,)), ((), ())), preferred_element_type=F32)


def dot_nt(a, b):
    return lax.dot_general(a, b, (((1,), (1,)), ((), ())), preferred_element_type=F32)


def dot_tn(a, b):
    return lax.dot_general(a, b, (((0,), (0,)), ((), ())), preferred_element_type=F32)


def attend(q, k, v, g, allowed):
    s = jnp.where(allowed, dot_nt(q, k) * SCALE, NEG)
    e = jnp.exp(s - jnp.max(s, axis=-1, keepdims=True))
    p = e * (1.0 / jnp.sum(e, axis=-1, keepdims=True))
    w = p.astype(BF)
    out = dot_nn(w, v)
    dp = dot_nt(g, v)
    delta = jnp.sum(p * dp, axis=-1, keepdims=True)
    ds = (p * (dp - delta) * SCALE).astype(BF)
    return out, dot_nn(ds, k), dot_tn(ds, q), dot_tn(w, g)


def kernel(
    own_hbm, slot_hbm, q_hbm, g_hbm, k_hbm, v_hbm, ek_hbm, ev_hbm,
    att, qg, kg, vg, ekg, evg,
    own_ref, slot_ref, q, g, k, v, ek, ev, sem_in,
    send_a, recv_a, send_b, recv_b, tab_a, tab_b, g1, g2, g3, g4,
    halo, back_send, back_recv, kacc, vacc, oacc, qacc, kmat, vmat, sel,
    send1, recv1, send2, recv2, send3, recv3, send4, recv4,
    sem_i, sem_h, s1, r1, s2, r2, s3, r3, s4, r4,
):
    me = lax.axis_index("seq")
    t = lax.axis_index("tp")
    x = lax.div(me, 16)
    z = lax.rem(lax.div(me, 4), 4)
    y = lax.rem(me, 4)

    def device(dx, dz, dy, dt):
        return (
            lax.rem(x + dx, 4) * 16 + lax.rem(z + dz, 4) * 4 + lax.rem(y + dy, 4),
            lax.rem(t + dt, 4),
        )

    def seq_peer(d):
        return device(lax.div(d, 16), lax.rem(lax.div(d, 4), 4), lax.rem(d, 4), 0)

    sources = (own_hbm, slot_hbm, k_hbm, v_hbm, q_hbm, g_hbm, ek_hbm, ev_hbm)
    places = (own_ref, slot_ref, k, v, q, g, ek, ev)
    loads = [pltpu.make_async_copy(a, b, sem_in.at[n]) for n, (a, b) in enumerate(zip(sources, places))]
    for load in loads:
        load.start()

    barrier = pltpu.get_barrier_semaphore()

    def greet(d, c):
        pl.semaphore_signal(barrier, 1, device_id=seq_peer(d), device_id_type=MESH)
        return c

    lax.fori_loop(1, 64, greet, 0)
    for dz in range(4):
        for dt in range(1, 4):
            pl.semaphore_signal(barrier, 1, device_id=device(0, dz, 0, dt), device_id_type=MESH)

    loads[0].wait()
    loads[1].wait()

    lane = lax.broadcasted_iota(I32, (1, 128), 1)
    owners = [own_ref[i // 4, i % 4] for i in range(16)]
    slots = [slot_ref[i // 4, i % 4] for i in range(16)]
    row_a = jnp.full((1, 128), -1, I32)
    row_b = jnp.zeros((1, 128), I32)
    row_c = jnp.zeros((1, 128), I32)
    for i in range(16):
        rank = jnp.int32(0)
        for j in range(i):
            rank = rank + (owners[j] == owners[i]).astype(I32)
        place = owners[i] * 2 + rank
        row_a = jnp.where(lane == place, slots[i], row_a)
        row_b = jnp.where(lane == place, i, row_b)
        row_c = jnp.where(lane == i, place, row_c)
        zo = lax.rem(lax.div(owners[i], 4), 4)
        g3[i] = lax.rem(z - zo + 4, 4) * 16 + i
    send_a[0] = row_a
    recv_a[0] = row_a
    rows_bc = jnp.concatenate([row_b, row_c], 0)
    send_b[0] = rows_bc
    recv_b[0] = rows_bc

    def self_block(b, hh):
        cols = pl.ds(pl.multiple_of(hh * 128, 128), 128)
        rows = pl.ds(128 * b, 128)
        if b == 0:
            kk = jnp.concatenate([halo[0, :, cols], k[0:128, cols]], 0)
            vv = jnp.concatenate([halo[1, :, cols], v[0:128, cols]], 0)
        else:
            kk, vv = k[:, cols], v[:, cols]
        heads = [pl.ds(pl.multiple_of(hh * 512 + 128 * u, 128), 128) for u in range(4)]
        qq = jnp.concatenate([q[rows, h] for h in heads], 0)
        gg = jnp.concatenate([g[rows, h] for h in heads], 0)
        r = lax.rem(lax.broadcasted_iota(I32, (512, 256), 0), 128)
        c = lax.broadcasted_iota(I32, (512, 256), 1)
        allowed = (c > r) & (c <= r + 128)
        if b == 0:
            allowed = allowed & (c >= jnp.where(me > 0, 0, 128))
        out, dq, dk, dv = attend(qq, kk, vv, gg, allowed)
        for u in range(4):
            oacc[rows, heads[u]] = out[128 * u : 128 * u + 128]
            qacc[rows, heads[u]] = dq[128 * u : 128 * u + 128]
        if b == 1:
            kacc[:, cols] = dk
            vacc[:, cols] = dv
        else:
            back_send[0, :, cols] = dk[0:128].astype(BF)
            back_send[1, :, cols] = dv[0:128].astype(BF)
            kacc[0:128, cols] = kacc[0:128, cols] + dk[128:256]
            vacc[0:128, cols] = vacc[0:128, cols] + dv[128:256]

    for n in range(2, 6):
        loads[n].wait()
    self_block(1, 0)

    pl.semaphore_wait(barrier, 75)

    nxt = (lax.rem(me + 1, 64), t)
    prv = (lax.rem(me + 63, 64), t)

    def remote(src, dst, ssem, rsem, dev):
        return pltpu.make_async_remote_copy(
            src_ref=src, dst_ref=dst, send_sem=ssem, recv_sem=rsem,
            device_id=dev, device_id_type=MESH,
        )

    def await_bytes(ref, sem):
        pltpu.make_async_copy(ref, ref, sem).wait()

    def tell(d, c):
        remote(send_a.at[0], recv_a.at[d], sem_i.at[0], sem_i.at[1], seq_peer(d)).start()
        return c

    lax.fori_loop(1, 64, tell, 0)
    for dz in range(1, 4):
        remote(send_b.at[0], recv_b.at[dz], sem_i.at[2], sem_i.at[3], device(0, dz, 0, 0)).start()
    halo_k = remote(k.at[pl.ds(128, 128)], halo.at[0], sem_h.at[0], sem_h.at[1], nxt)
    halo_v = remote(v.at[pl.ds(128, 128)], halo.at[1], sem_h.at[2], sem_h.at[3], nxt)
    halo_k.start()
    halo_v.start()
    self_block(1, 1)
    loads[6].wait()
    loads[7].wait()

    await_bytes(recv_a.at[pl.ds(1, 63)], sem_i.at[1])
    await_bytes(recv_b.at[pl.ds(1, 3)], sem_i.at[3])
    copy_a = pltpu.make_async_copy(recv_a, tab_a, sem_i.at[4])
    copy_b = pltpu.make_async_copy(recv_b, tab_b, sem_i.at[5])
    copy_a.start()
    copy_b.start()
    copy_a.wait()
    copy_b.wait()

    def fill1(d, c):
        dx, dy = lax.div(d, 4), lax.rem(d, 4)
        for dz in range(4):
            src = lax.rem(4 - dx, 4) * 16 + ((4 - dz) % 4) * 4 + lax.rem(4 - dy, 4)
            for rank in range(2):
                g1[d * 8 + dz * 2 + rank] = jnp.maximum(tab_a[src, 0, 2 * me + rank], 0)
        return c

    lax.fori_loop(0, 16, fill1, 0)

    def plane_peer(d):
        return device(lax.div(d, 4), 0, lax.rem(d, 4), 0)

    def stage1(c):
        store = (ek, ev)[c // 4]
        tt = lax.rem(t + c % 4, 4)
        for m in range(8):
            recv1[c][m] = store[g1[m], tt]

        def gather(d, carry):
            for m in range(8):
                send1[c][d * 8 + m] = store[g1[d * 8 + m], tt]
            return carry

        lax.fori_loop(1, 16, gather, 0)

        def start(d, carry):
            part = pl.ds(d * 8, 8)
            remote(send1[c].at[part], recv1[c].at[part], s1.at[c], r1.at[c], plane_peer(d)).start()
            return carry

        lax.fori_loop(1, 16, start, 0)

    def stage2(c):
        kv, dt = c // 4, c % 4
        low = 1 if dt == 0 else 0
        await_bytes(recv1[c].at[pl.ds(8, 120)], r1.at[c])
        if dt == 0:
            for i in range(16):
                recv2[kv][i] = recv1[c][g2[i]]

        def gather(dz, carry):
            for i in range(16):
                send2[c][dz * 16 + i] = recv1[c][g2[dz * 16 + i]]
            return carry

        lax.fori_loop(low, 4, gather, 0)
        for dz in range(low, 4):
            remote(
                send2[c].at[pl.ds(dz * 16, 16)],
                recv2[kv].at[pl.ds(dt * 64 + dz * 16, 16)],
                s2.at[c], r2.at[c], device(0, dz, 0, dt),
            ).start()

    for c in range(AHEAD):
        stage1(c)

    def fill2(i, c):
        for dz in range(4):
            place = tab_b[(4 - dz) % 4, 1, i]
            owner, rank = lax.div(place, 2), lax.rem(place, 2)
            ox, oy = lax.div(owner, 16), lax.rem(owner, 4)
            dx, dy = lax.rem(x - ox + 4, 4), lax.rem(y - oy + 4, 4)
            g2[dz * 16 + i] = (dx * 4 + dy) * 8 + dz * 2 + rank
        return c

    lax.fori_loop(0, 16, fill2, 0)

    def fill4(d, c):
        dx, dy = lax.div(d, 4), lax.rem(d, 4)
        owner = lax.rem(x + dx, 4) * 16 + z * 4 + lax.rem(y + dy, 4)
        for dz in range(4):
            for rank in range(2):
                g4[d * 8 + dz * 2 + rank] = dz * 16 + tab_b[dz, 0, owner * 2 + rank]
        return c

    lax.fori_loop(0, 16, fill4, 0)

    row_at = lax.broadcasted_iota(I32, (512, 128), 0)
    for w in range(8):
        want = jnp.full((1, 128), -1, I32)
        for n in range(16):
            p = w * 16 + n
            d, dz, rank = p // 8, (p // 2) % 4, p % 2
            got = tab_a[(d // 4) * 16 + dz * 4 + d % 4, 0, 2 * me + rank]
            want = jnp.where(lax.div(lane, 8) == n, got * 8 + lax.rem(lane, 8), want)
        sel[:, pl.ds(128 * w, 128)] = jnp.where(row_at == want, 1.0, 0.0).astype(BF)

    halo_k.wait()
    halo_v.wait()
    self_block(0, 0)
    back_k = remote(back_send.at[0], back_recv.at[0], sem_h.at[4], sem_h.at[5], prv)
    back_v = remote(back_send.at[1], back_recv.at[1], sem_h.at[6], sem_h.at[7], prv)
    for c in range(8):
        if c + AHEAD < 8:
            stage1(c + AHEAD)
        stage2(c)
        if c == 1:
            self_block(0, 1)
            back_k.start()
            back_v.start()

    for kv in range(2):
        for dt in range(4):
            low = 16 if dt == 0 else 0
            await_bytes(recv2[kv].at[pl.ds(dt * 64 + low, 64 - low)], r2.at[kv * 4 + dt])
        mat = (kmat, vmat)[kv]
        for i in range(16):
            for dt in range(4):
                mat[pl.ds(i * 32 + dt * 8, 8), :] = recv2[kv][g3[i] + dt * 64]

    def cross(cc, carry):
        rows = pl.ds(pl.multiple_of(cc * 64, 64), 64)
        near = pl.ds(pl.multiple_of(cc * 128, 128), 128)
        qq = jnp.concatenate([q[rows, 128 * h : 128 * h + 128] for h in range(8)], 0)
        gg = jnp.concatenate([g[rows, 128 * h : 128 * h + 128] for h in range(8)], 0)
        r = lax.broadcasted_iota(I32, (512, 128), 0)
        n = lax.broadcasted_iota(I32, (512, 128), 1)
        allowed = lax.div(r, 256) == lax.div(lax.rem(n, 8), 4)
        out, dq, dk, dv = attend(qq, kmat[near, :], vmat[near, :], gg, allowed)
        for h in range(8):
            cols = pl.ds(128 * h, 128)
            att[rows, cols] = (oacc[rows, cols] + out[64 * h : 64 * h + 64]).astype(BF)
            qg[rows, cols] = (qacc[rows, cols] + dq[64 * h : 64 * h + 64]).astype(BF)
        for kv in range(2):
            tiles = (dk, dv)[kv].astype(BF).reshape(16, 8, 128)
            for j in range(4):
                for dt in range(4):
                    send3[kv][dt * 16 + cc * 4 + j] = tiles[j * 4 + dt]
                recv3[kv * 4][cc * 4 + j] = tiles[j * 4]
        return carry

    lax.fori_loop(0, 4, cross, 0)

    def stage3(c):
        kv, dt = c // 4, c % 4
        for dz in range(1 if dt == 0 else 0, 4):
            remote(
                send3[kv].at[pl.ds(dt * 16, 16)],
                recv3[c].at[pl.ds(dz * 16, 16)],
                s3.at[c], r3.at[c], device(0, dz, 0, (4 - dt) % 4),
            ).start()

    def stage4(c):
        low = 16 if c % 4 == 0 else 0
        await_bytes(recv3[c].at[pl.ds(low, 64 - low)], r3.at[c])
        for m in range(8):
            recv4[c][m] = recv3[c][g4[m]]

        def gather(d, carry):
            for m in range(8):
                send4[c][d * 8 + m] = recv3[c][g4[d * 8 + m]]
            return carry

        lax.fori_loop(1, 16, gather, 0)

        def start(d, carry):
            part = pl.ds(d * 8, 8)
            remote(send4[c].at[part], recv4[c].at[part], s4.at[c], r4.at[c], plane_peer(d)).start()
            return carry

        lax.fori_loop(1, 16, start, 0)

    def gather_store(c):
        await_bytes(recv4[c].at[pl.ds(8, 120)], r4.at[c])
        total = dot_nn(sel[...], recv4[c].reshape(1024, 128)[...])
        (ekg, evg)[c // 4][:, lax.rem(t + c % 4, 4)] = total.reshape(64, 8, 128).astype(BF)

    for c in range(AHEAD):
        stage3(c)

    back_k.wait()
    back_v.wait()
    kg[0:128, :] = kacc[0:128, :].astype(BF)
    vg[0:128, :] = vacc[0:128, :].astype(BF)
    kg[128:256, :] = (kacc[128:256, :] + back_recv[0].astype(F32)).astype(BF)
    vg[128:256, :] = (vacc[128:256, :] + back_recv[1].astype(F32)).astype(BF)

    for c in range(8 + LAG):
        if c < 8:
            if c + AHEAD < 8:
                stage3(c + AHEAD)
            stage4(c)
        if c >= LAG:
            gather_store(c - LAG)

    await_bytes(recv_a.at[pl.ds(1, 63)], sem_i.at[0])
    await_bytes(recv_b.at[pl.ds(1, 3)], sem_i.at[2])
    for c in range(8):
        low = 16 if c % 4 == 0 else 0
        await_bytes(send1[c].at[pl.ds(8, 120)], s1.at[c])
        await_bytes(send2[c].at[pl.ds(low, 64 - low)], s2.at[c])
        await_bytes(recv3[c].at[pl.ds(low, 64 - low)], s3.at[c])
        await_bytes(send4[c].at[pl.ds(8, 120)], s4.at[c])


def write_out(*refs):
    copies = [pltpu.make_async_copy(refs[n], refs[6 + n], refs[12].at[n]) for n in range(6)]
    for copy in copies:
        copy.start()
    for copy in copies:
        copy.wait()


def tiles(n):
    return pltpu.VMEM((n, 8, 128), BF)


def body(queries, seq_keys, seq_values, out_grad, enc_keys, enc_values, nbr_owner, nbr_slot):
    def to_tiles(e):
        return e.reshape(64, 4, 4, 2, 128).transpose(0, 2, 3, 1, 4).reshape(64, 4, 8, 128)

    def from_tiles(e):
        return e.reshape(64, 4, 2, 4, 128).transpose(0, 3, 1, 2, 4).reshape(64, 4, 1024)

    hbm = pl.BlockSpec(memory_space=pltpu.HBM)
    vmem = pl.BlockSpec(memory_space=pltpu.VMEM)
    dma = pltpu.SemaphoreType.DMA
    outs = pl.pallas_call(
        kernel,
        out_shape=(
            jax.ShapeDtypeStruct((256, 1024), BF),
            jax.ShapeDtypeStruct((256, 1024), BF),
            jax.ShapeDtypeStruct((256, 256), BF),
            jax.ShapeDtypeStruct((256, 256), BF),
            jax.ShapeDtypeStruct((64, 4, 8, 128), BF),
            jax.ShapeDtypeStruct((64, 4, 8, 128), BF),
        ),
        in_specs=[hbm] * 8,
        out_specs=(vmem,) * 6,
        scratch_shapes=[
            pltpu.SMEM((4, 4), I32),
            pltpu.SMEM((4, 4), I32),
            pltpu.VMEM((256, 1024), BF),
            pltpu.VMEM((256, 1024), BF),
            pltpu.VMEM((256, 256), BF),
            pltpu.VMEM((256, 256), BF),
            pltpu.VMEM((64, 4, 8, 128), BF),
            pltpu.VMEM((64, 4, 8, 128), BF),
            dma((8,)),
            pltpu.VMEM((1, 1, 128), I32),
            pltpu.VMEM((64, 1, 128), I32),
            pltpu.VMEM((1, 2, 128), I32),
            pltpu.VMEM((4, 2, 128), I32),
            pltpu.SMEM((64, 1, 128), I32),
            pltpu.SMEM((4, 2, 128), I32),
            pltpu.SMEM((128,), I32),
            pltpu.SMEM((64,), I32),
            pltpu.SMEM((16,), I32),
            pltpu.SMEM((128,), I32),
            pltpu.VMEM((2, 128, 256), BF),
            pltpu.VMEM((2, 128, 256), BF),
            pltpu.VMEM((2, 128, 256), BF),
            pltpu.VMEM((256, 256), F32),
            pltpu.VMEM((256, 256), F32),
            pltpu.VMEM((256, 1024), F32),
            pltpu.VMEM((256, 1024), F32),
            pltpu.VMEM((512, 128), BF),
            pltpu.VMEM((512, 128), BF),
            pltpu.VMEM((512, 1024), BF),
            [tiles(128)] * 8,
            [tiles(128)] * 8,
            [tiles(64)] * 8,
            [tiles(256)] * 2,
            [tiles(64)] * 2,
            [tiles(64)] * 8,
            [tiles(128)] * 8,
            [tiles(128)] * 8,
            dma((6,)),
            dma((8,)),
            dma((8,)),
            dma((8,)),
            dma((8,)),
            dma((8,)),
            dma((8,)),
            dma((8,)),
            dma((8,)),
            dma((8,)),
        ],
        compiler_params=pltpu.CompilerParams(
            collective_id=0, has_side_effects=True, vmem_limit_bytes=VMEM_MAIN
        ),
        name="retro",
    )(
        *[pltpu.with_memory_space_constraint(a, pltpu.HBM) for a in (
            nbr_owner, nbr_slot, queries, out_grad, seq_keys, seq_values,
            to_tiles(enc_keys), to_tiles(enc_values))]
    )
    outs = pl.pallas_call(
        write_out,
        out_shape=tuple(jax.ShapeDtypeStruct(o.shape, BF) for o in outs),
        in_specs=[pl.BlockSpec(memory_space=pl.ANY)] * 6,
        out_specs=(hbm,) * 6,
        scratch_shapes=[dma((6,))],
        compiler_params=pltpu.CompilerParams(vmem_limit_bytes=1 << 20),
        name="write_out",
    )(*outs)
    att, qg, kg, vg, ekg, evg = outs
    return att, qg, kg, vg, from_tiles(ekg), from_tiles(evg)


def solution(mesh):
    shard = P("seq", "tp")
    store = P("seq", "tp", None)
    return jax.shard_map(
        body,
        mesh=mesh,
        in_specs=(shard, shard, shard, shard, store, store, P("seq", None), P("seq", None)),
        out_specs=(shard, shard, shard, shard, store, store),
        check_vma=False,
    )
```

```python
import math

import jax
import jax.numpy as jnp
from jax import lax
from jax.experimental import pallas as pl
from jax.experimental.pallas import tpu as pltpu
from jax.sharding import PartitionSpec as P

HEAD = 128
GROUP = 4
SCALE = 1.0 / math.sqrt(HEAD)
NEG = -1e30
AHEAD = 3
VMEM_MAIN = 48 << 20
LAG = 3
PLANE = tuple(range(1, 16))
MESH = pl.DeviceIdType.MESH
BF = jnp.bfloat16
F32 = jnp.float32
I32 = jnp.int32


def dot_nn(a, b):
    return lax.dot_general(a, b, (((1,), (0,)), ((), ())), preferred_element_type=F32)


def dot_nt(a, b):
    return lax.dot_general(a, b, (((1,), (1,)), ((), ())), preferred_element_type=F32)


def dot_tn(a, b):
    return lax.dot_general(a, b, (((0,), (0,)), ((), ())), preferred_element_type=F32)


def probs(q, k, allowed):
    s = jnp.where(allowed, dot_nt(q, k) * SCALE, NEG)
    e = jnp.exp(s - jnp.max(s, axis=-1, keepdims=True))
    return e * (1.0 / jnp.sum(e, axis=-1, keepdims=True))


def score_grads(p, v, g):
    dp = dot_nt(g, v)
    delta = jnp.sum(p * dp, axis=-1, keepdims=True)
    return (p * (dp - delta) * SCALE).astype(BF)


def attend(q, k, v, g, allowed):
    p = probs(q, k, allowed)
    w = p.astype(BF)
    ds = score_grads(p, v, g)
    return dot_nn(w, v), dot_nn(ds, k), dot_tn(ds, q), dot_tn(w, g)


def kernel(
    own_hbm, slot_hbm, q_hbm, g_hbm, k_hbm, v_hbm, ek_hbm, ev_hbm,
    att, qg, kg, vg, ekg, evg,
    own_ref, slot_ref, q, g, k, v, ek, ev, sem_in,
    send_a, recv_a, send_b, recv_b, tab_a, tab_b, g1, g2, g3, g4,
    pbuf, halo, back_send, back_recv, kacc, vacc, oacc, qacc, kmat, vmat, sel,
    send1, recv1, send2, recv2, send3, recv3, send4, recv4,
    sem_i, sem_h, s1, r1, s2, r2, s3, r3, s4, r4,
):
    me = lax.axis_index("seq")
    t = lax.axis_index("tp")
    x = lax.div(me, 16)
    z = lax.rem(lax.div(me, 4), 4)
    y = lax.rem(me, 4)

    def device(dx, dz, dy, dt):
        return (
            lax.rem(x + dx, 4) * 16 + lax.rem(z + dz, 4) * 4 + lax.rem(y + dy, 4),
            lax.rem(t + dt, 4),
        )

    def seq_peer(d):
        return device(lax.div(d, 16), lax.rem(lax.div(d, 4), 4), lax.rem(d, 4), 0)

    sources = (own_hbm, slot_hbm, k_hbm, v_hbm, q_hbm, g_hbm, ek_hbm, ev_hbm)
    places = (own_ref, slot_ref, k, v, q, g, ek, ev)
    loads = [pltpu.make_async_copy(a, b, sem_in.at[n]) for n, (a, b) in enumerate(zip(sources, places))]
    for load in loads:
        load.start()

    barrier = pltpu.get_barrier_semaphore()

    def greet(d, c):
        pl.semaphore_signal(barrier, 1, device_id=seq_peer(d), device_id_type=MESH)
        return c

    lax.fori_loop(1, 64, greet, 0)
    for dz in range(4):
        for dt in range(1, 4):
            pl.semaphore_signal(barrier, 1, device_id=device(0, dz, 0, dt), device_id_type=MESH)

    loads[0].wait()
    loads[1].wait()

    lane = lax.broadcasted_iota(I32, (1, 128), 1)
    owners = [own_ref[i // 4, i % 4] for i in range(16)]
    slots = [slot_ref[i // 4, i % 4] for i in range(16)]
    row_a = jnp.full((1, 128), -1, I32)
    row_b = jnp.zeros((1, 128), I32)
    row_c = jnp.zeros((1, 128), I32)
    for i in range(16):
        rank = jnp.int32(0)
        for j in range(i):
            rank = rank + (owners[j] == owners[i]).astype(I32)
        place = owners[i] * 2 + rank
        row_a = jnp.where(lane == place, slots[i], row_a)
        row_b = jnp.where(lane == place, i, row_b)
        row_c = jnp.where(lane == i, place, row_c)
        zo = lax.rem(lax.div(owners[i], 4), 4)
        g3[i] = lax.rem(z - zo + 4, 4) * 16 + i
    send_a[0] = row_a
    recv_a[0] = row_a
    rows_bc = jnp.concatenate([row_b, row_c], 0)
    send_b[0] = rows_bc
    recv_b[0] = rows_bc

    def self_block(b, hh):
        cols = pl.ds(pl.multiple_of(hh * 128, 128), 128)
        rows = pl.ds(128 * b, 128)
        if b == 0:
            kk = jnp.concatenate([halo[0, :, cols], k[0:128, cols]], 0)
            vv = jnp.concatenate([halo[1, :, cols], v[0:128, cols]], 0)
        else:
            kk, vv = k[:, cols], v[:, cols]
        heads = [pl.ds(pl.multiple_of(hh * 512 + 128 * u, 128), 128) for u in range(4)]
        qq = jnp.concatenate([q[rows, h] for h in heads], 0)
        gg = jnp.concatenate([g[rows, h] for h in heads], 0)
        r = lax.rem(lax.broadcasted_iota(I32, (512, 256), 0), 128)
        c = lax.broadcasted_iota(I32, (512, 256), 1)
        allowed = (c > r) & (c <= r + 128)
        if b == 0:
            allowed = allowed & (c >= jnp.where(me > 0, 0, 128))
        out, dq, dk, dv = attend(qq, kk, vv, gg, allowed)
        for u in range(4):
            oacc[rows, heads[u]] = out[128 * u : 128 * u + 128]
            qacc[rows, heads[u]] = dq[128 * u : 128 * u + 128]
        if b == 1:
            kacc[:, cols] = dk
            vacc[:, cols] = dv
        else:
            back_send[0, :, cols] = dk[0:128].astype(BF)
            back_send[1, :, cols] = dv[0:128].astype(BF)
            kacc[0:128, cols] = kacc[0:128, cols] + dk[128:256]
            vacc[0:128, cols] = vacc[0:128, cols] + dv[128:256]

    pl.semaphore_wait(barrier, 75)

    nxt = (lax.rem(me + 1, 64), t)
    prv = (lax.rem(me + 63, 64), t)

    def remote(src, dst, ssem, rsem, dev):
        return pltpu.make_async_remote_copy(
            src_ref=src, dst_ref=dst, send_sem=ssem, recv_sem=rsem,
            device_id=dev, device_id_type=MESH,
        )

    def await_bytes(ref, sem):
        pltpu.make_async_copy(ref, ref, sem).wait()

    def tell(d, c):
        remote(send_a.at[0], recv_a.at[d], sem_i.at[0], sem_i.at[1], seq_peer(d)).start()
        return c

    lax.fori_loop(1, 64, tell, 0)
    for dz in range(1, 4):
        remote(send_b.at[0], recv_b.at[dz], sem_i.at[2], sem_i.at[3], device(0, dz, 0, 0)).start()
    for n in range(2, 6):
        loads[n].wait()
    halo_k = remote(k.at[pl.ds(128, 128)], halo.at[0], sem_h.at[0], sem_h.at[1], nxt)
    halo_v = remote(v.at[pl.ds(128, 128)], halo.at[1], sem_h.at[2], sem_h.at[3], nxt)
    halo_k.start()
    halo_v.start()
    self_block(1, 0)
    self_block(1, 1)
    loads[6].wait()
    loads[7].wait()

    await_bytes(recv_a.at[pl.ds(1, 63)], sem_i.at[1])
    await_bytes(recv_b.at[pl.ds(1, 3)], sem_i.at[3])
    copy_a = pltpu.make_async_copy(recv_a, tab_a, sem_i.at[4])
    copy_b = pltpu.make_async_copy(recv_b, tab_b, sem_i.at[5])
    copy_a.start()
    copy_b.start()
    copy_a.wait()
    copy_b.wait()

    def fill1(d, c):
        dx, dy = lax.div(d, 4), lax.rem(d, 4)
        for dz in range(4):
            src = lax.rem(4 - dx, 4) * 16 + ((4 - dz) % 4) * 4 + lax.rem(4 - dy, 4)
            for rank in range(2):
                g1[d * 8 + dz * 2 + rank] = jnp.maximum(tab_a[src, 0, 2 * me + rank], 0)
        return c

    lax.fori_loop(0, 16, fill1, 0)

    def plane_peer(d):
        return device(d // 4, 0, d % 4, 0)

    def stage1(c):
        store = (ek, ev)[c // 4]
        tt = lax.rem(t + c % 4, 4)
        for m in range(8):
            recv1[c][m] = store[g1[m], tt]

        def gather(d, carry):
            for m in range(8):
                send1[c][d * 8 + m] = store[g1[d * 8 + m], tt]
            return carry

        lax.fori_loop(1, 16, gather, 0)

        for d in PLANE:
            part = pl.ds(d * 8, 8)
            remote(send1[c].at[part], recv1[c].at[part], s1.at[c], r1.at[c], plane_peer(d)).start()

    def stage2(c):
        kv, dt = c // 4, c % 4
        low = 1 if dt == 0 else 0
        await_bytes(recv1[c].at[pl.ds(8, 120)], r1.at[c])
        if dt == 0:
            for i in range(16):
                recv2[kv][i] = recv1[c][g2[i]]

        def gather(dz, carry):
            for i in range(16):
                send2[c][dz * 16 + i] = recv1[c][g2[dz * 16 + i]]
            return carry

        lax.fori_loop(low, 4, gather, 0)
        for dz in range(low, 4):
            remote(
                send2[c].at[pl.ds(dz * 16, 16)],
                recv2[kv].at[pl.ds(dt * 64 + dz * 16, 16)],
                s2.at[c], r2.at[c], device(0, dz, 0, dt),
            ).start()

    for c in range(AHEAD):
        stage1(c)

    def fill2(i, c):
        for dz in range(4):
            place = tab_b[(4 - dz) % 4, 1, i]
            owner, rank = lax.div(place, 2), lax.rem(place, 2)
            ox, oy = lax.div(owner, 16), lax.rem(owner, 4)
            dx, dy = lax.rem(x - ox + 4, 4), lax.rem(y - oy + 4, 4)
            g2[dz * 16 + i] = (dx * 4 + dy) * 8 + dz * 2 + rank
        return c

    lax.fori_loop(0, 16, fill2, 0)

    def fill4(d, c):
        dx, dy = lax.div(d, 4), lax.rem(d, 4)
        owner = lax.rem(x + dx, 4) * 16 + z * 4 + lax.rem(y + dy, 4)
        for dz in range(4):
            for rank in range(2):
                g4[d * 8 + dz * 2 + rank] = dz * 16 + tab_b[dz, 0, owner * 2 + rank]
        return c

    lax.fori_loop(0, 16, fill4, 0)

    row_at = lax.broadcasted_iota(I32, (512, 128), 0)
    for w in range(8):
        want = jnp.full((1, 128), -1, I32)
        for n in range(16):
            p = w * 16 + n
            d, dz, rank = p // 8, (p // 2) % 4, p % 2
            got = tab_a[(d // 4) * 16 + dz * 4 + d % 4, 0, 2 * me + rank]
            want = jnp.where(lax.div(lane, 8) == n, got * 8 + lax.rem(lane, 8), want)
        sel[:, pl.ds(128 * w, 128)] = jnp.where(row_at == want, 1.0, 0.0).astype(BF)

    halo_k.wait()
    halo_v.wait()
    self_block(0, 0)
    back_k = remote(back_send.at[0], back_recv.at[0], sem_h.at[4], sem_h.at[5], prv)
    back_v = remote(back_send.at[1], back_recv.at[1], sem_h.at[6], sem_h.at[7], prv)
    for c in range(8):
        if c + AHEAD < 8:
            stage1(c + AHEAD)
        stage2(c)
        if c == 1:
            self_block(0, 1)
            back_k.start()
            back_v.start()

    def collect(kv):
        for dt in range(4):
            low = 16 if dt == 0 else 0
            await_bytes(recv2[kv].at[pl.ds(dt * 64 + low, 64 - low)], r2.at[kv * 4 + dt])
        mat = (kmat, vmat)[kv]
        for i in range(16):
            for dt in range(4):
                mat[pl.ds(i * 32 + dt * 8, 8), :] = recv2[kv][g3[i] + dt * 64]

    def stretch(ref, cc):
        rows = pl.ds(pl.multiple_of(cc * 64, 64), 64)
        return jnp.concatenate([ref[rows, 128 * h : 128 * h + 128] for h in range(8)], 0)

    def hand_back(kv, cc, grad):
        parts = grad.astype(BF).reshape(16, 8, 128)
        for j in range(4):
            for dt in range(4):
                send3[kv][dt * 16 + cc * 4 + j] = parts[j * 4 + dt]
            recv3[kv * 4][cc * 4 + j] = parts[j * 4]

    def cross_keys(cc, carry):
        near = pl.ds(pl.multiple_of(cc * 128, 128), 128)
        r = lax.broadcasted_iota(I32, (512, 128), 0)
        n = lax.broadcasted_iota(I32, (512, 128), 1)
        allowed = lax.div(r, 256) == lax.div(lax.rem(n, 8), 4)
        p = probs(stretch(q, cc), kmat[near, :], allowed)
        pbuf[cc] = p
        hand_back(1, cc, dot_tn(p.astype(BF), stretch(g, cc)))
        return carry

    def cross_values(cc, carry):
        rows = pl.ds(pl.multiple_of(cc * 64, 64), 64)
        near = pl.ds(pl.multiple_of(cc * 128, 128), 128)
        p = pbuf[cc]
        ds = score_grads(p, vmat[near, :], stretch(g, cc))
        hand_back(0, cc, dot_tn(ds, stretch(q, cc)))
        out = dot_nn(p.astype(BF), vmat[near, :])
        dq = dot_nn(ds, kmat[near, :])
        for h in range(8):
            cols = pl.ds(128 * h, 128)
            att[rows, cols] = (oacc[rows, cols] + out[64 * h : 64 * h + 64]).astype(BF)
            qg[rows, cols] = (qacc[rows, cols] + dq[64 * h : 64 * h + 64]).astype(BF)
        return carry

    def stage3(c):
        kv, dt = c // 4, c % 4
        for dz in range(1 if dt == 0 else 0, 4):
            remote(
                send3[kv].at[pl.ds(dt * 16, 16)],
                recv3[c].at[pl.ds(dz * 16, 16)],
                s3.at[c], r3.at[c], device(0, dz, 0, (4 - dt) % 4),
            ).start()

    def stage4(c):
        low = 16 if c % 4 == 0 else 0
        await_bytes(recv3[c].at[pl.ds(low, 64 - low)], r3.at[c])
        for m in range(8):
            recv4[c][m] = recv3[c][g4[m]]

        def gather(d, carry):
            for m in range(8):
                send4[c][d * 8 + m] = recv3[c][g4[d * 8 + m]]
            return carry

        lax.fori_loop(1, 16, gather, 0)

        for d in PLANE:
            part = pl.ds(d * 8, 8)
            remote(send4[c].at[part], recv4[c].at[part], s4.at[c], r4.at[c], plane_peer(d)).start()

    def gather_store(c):
        await_bytes(recv4[c].at[pl.ds(8, 120)], r4.at[c])
        total = dot_nn(sel[...], recv4[c].reshape(1024, 128)[...])
        (ekg, evg)[c // 4][:, lax.rem(t + c % 4, 4)] = total.reshape(64, 8, 128).astype(BF)

    collect(0)
    lax.fori_loop(0, 4, cross_keys, 0)
    for c in range(4, 8):
        stage3(c)
    collect(1)
    lax.fori_loop(0, 4, cross_values, 0)
    for c in range(4):
        stage3(c)

    def window_grads():
        back_k.wait()
        back_v.wait()
        kg[0:128, :] = kacc[0:128, :].astype(BF)
        vg[0:128, :] = vacc[0:128, :].astype(BF)
        kg[128:256, :] = (kacc[128:256, :] + back_recv[0].astype(F32)).astype(BF)
        vg[128:256, :] = (vacc[128:256, :] + back_recv[1].astype(F32)).astype(BF)

    order = (4, 5, 6, 7, 0, 1, 2, 3)
    for n in range(8 + LAG):
        if n < 8:
            stage4(order[n])
        if n == 1:
            window_grads()
        if n >= LAG:
            gather_store(order[n - LAG])

    await_bytes(recv_a.at[pl.ds(1, 63)], sem_i.at[0])
    await_bytes(recv_b.at[pl.ds(1, 3)], sem_i.at[2])
    for c in range(8):
        low = 16 if c % 4 == 0 else 0
        await_bytes(send1[c].at[pl.ds(8, 120)], s1.at[c])
        await_bytes(send2[c].at[pl.ds(low, 64 - low)], s2.at[c])
        await_bytes(recv3[c].at[pl.ds(low, 64 - low)], s3.at[c])
        await_bytes(send4[c].at[pl.ds(8, 120)], s4.at[c])


def write_out(*refs):
    copies = [pltpu.make_async_copy(refs[n], refs[6 + n], refs[12].at[n]) for n in range(6)]
    for copy in copies:
        copy.start()
    for copy in copies:
        copy.wait()


def tiles(n):
    return pltpu.VMEM((n, 8, 128), BF)


def body(queries, seq_keys, seq_values, out_grad, enc_keys, enc_values, nbr_owner, nbr_slot):
    def to_tiles(e):
        return e.reshape(64, 4, 4, 2, 128).transpose(0, 2, 3, 1, 4).reshape(64, 4, 8, 128)

    def from_tiles(e):
        return e.reshape(64, 4, 2, 4, 128).transpose(0, 3, 1, 2, 4).reshape(64, 4, 1024)

    hbm = pl.BlockSpec(memory_space=pltpu.HBM)
    vmem = pl.BlockSpec(memory_space=pltpu.VMEM)
    dma = pltpu.SemaphoreType.DMA
    outs = pl.pallas_call(
        kernel,
        out_shape=(
            jax.ShapeDtypeStruct((256, 1024), BF),
            jax.ShapeDtypeStruct((256, 1024), BF),
            jax.ShapeDtypeStruct((256, 256), BF),
            jax.ShapeDtypeStruct((256, 256), BF),
            jax.ShapeDtypeStruct((64, 4, 8, 128), BF),
            jax.ShapeDtypeStruct((64, 4, 8, 128), BF),
        ),
        in_specs=[hbm] * 8,
        out_specs=(vmem,) * 6,
        scratch_shapes=[
            pltpu.SMEM((4, 4), I32),
            pltpu.SMEM((4, 4), I32),
            pltpu.VMEM((256, 1024), BF),
            pltpu.VMEM((256, 1024), BF),
            pltpu.VMEM((256, 256), BF),
            pltpu.VMEM((256, 256), BF),
            pltpu.VMEM((64, 4, 8, 128), BF),
            pltpu.VMEM((64, 4, 8, 128), BF),
            dma((8,)),
            pltpu.VMEM((1, 1, 128), I32),
            pltpu.VMEM((64, 1, 128), I32),
            pltpu.VMEM((1, 2, 128), I32),
            pltpu.VMEM((4, 2, 128), I32),
            pltpu.SMEM((64, 1, 128), I32),
            pltpu.SMEM((4, 2, 128), I32),
            pltpu.SMEM((128,), I32),
            pltpu.SMEM((64,), I32),
            pltpu.SMEM((16,), I32),
            pltpu.SMEM((128,), I32),
            pltpu.VMEM((4, 512, 128), F32),
            pltpu.VMEM((2, 128, 256), BF),
            pltpu.VMEM((2, 128, 256), BF),
            pltpu.VMEM((2, 128, 256), BF),
            pltpu.VMEM((256, 256), F32),
            pltpu.VMEM((256, 256), F32),
            pltpu.VMEM((256, 1024), F32),
            pltpu.VMEM((256, 1024), F32),
            pltpu.VMEM((512, 128), BF),
            pltpu.VMEM((512, 128), BF),
            pltpu.VMEM((512, 1024), BF),
            [tiles(128)] * 8,
            [tiles(128)] * 8,
            [tiles(64)] * 8,
            [tiles(256)] * 2,
            [tiles(64)] * 2,
            [tiles(64)] * 8,
            [tiles(128)] * 8,
            [tiles(128)] * 8,
            dma((6,)),
            dma((8,)),
            dma((8,)),
            dma((8,)),
            dma((8,)),
            dma((8,)),
            dma((8,)),
            dma((8,)),
            dma((8,)),
            dma((8,)),
        ],
        compiler_params=pltpu.CompilerParams(
            collective_id=0, has_side_effects=True, vmem_limit_bytes=VMEM_MAIN
        ),
        name="retro",
    )(
        *[pltpu.with_memory_space_constraint(a, pltpu.HBM) for a in (
            nbr_owner, nbr_slot, queries, out_grad, seq_keys, seq_values,
            to_tiles(enc_keys), to_tiles(enc_values))]
    )
    outs = pl.pallas_call(
        write_out,
        out_shape=tuple(jax.ShapeDtypeStruct(o.shape, BF) for o in outs),
        in_specs=[pl.BlockSpec(memory_space=pl.ANY)] * 6,
        out_specs=(hbm,) * 6,
        scratch_shapes=[dma((6,))],
        compiler_params=pltpu.CompilerParams(vmem_limit_bytes=1 << 20),
        name="write_out",
    )(*outs)
    att, qg, kg, vg, ekg, evg = outs
    return att, qg, kg, vg, from_tiles(ekg), from_tiles(evg)


def solution(mesh):
    shard = P("seq", "tp")
    store = P("seq", "tp", None)
    return jax.shard_map(
        body,
        mesh=mesh,
        in_specs=(shard, shard, shard, shard, store, store, P("seq", None), P("seq", None)),
        out_specs=(shard, shard, shard, shard, store, store),
        check_vma=False,
    )
```

```python
import math

import jax
import jax.numpy as jnp
from jax import lax
from jax.experimental import pallas as pl
from jax.experimental.pallas import tpu as pltpu
from jax.sharding import PartitionSpec as P

HEAD = 128
GROUP = 4
SCALE = 1.0 / math.sqrt(HEAD)
NEG = -1e30
AHEAD = 3
VMEM_MAIN = 48 << 20
LAG = 3
PLANE = tuple(range(1, 16))
MESH = pl.DeviceIdType.MESH
BF = jnp.bfloat16
F32 = jnp.float32
I32 = jnp.int32


def dot_nn(a, b):
    return lax.dot_general(a, b, (((1,), (0,)), ((), ())), preferred_element_type=F32)


def dot_nt(a, b):
    return lax.dot_general(a, b, (((1,), (1,)), ((), ())), preferred_element_type=F32)


def dot_tn(a, b):
    return lax.dot_general(a, b, (((0,), (0,)), ((), ())), preferred_element_type=F32)


def probs(q, k, allowed):
    s = jnp.where(allowed, dot_nt(q, k) * SCALE, NEG)
    e = jnp.exp(s - jnp.max(s, axis=-1, keepdims=True))
    return e * (1.0 / jnp.sum(e, axis=-1, keepdims=True))


def score_grads(p, v, g):
    dp = dot_nt(g, v)
    delta = jnp.sum(p * dp, axis=-1, keepdims=True)
    return (p * (dp - delta) * SCALE).astype(BF)


def attend(q, k, v, g, allowed):
    p = probs(q, k, allowed)
    w = p.astype(BF)
    ds = score_grads(p, v, g)
    return dot_nn(w, v), dot_nn(ds, k), dot_tn(ds, q), dot_tn(w, g)


def kernel(
    own_hbm, slot_hbm, q_hbm, g_hbm, k_hbm, v_hbm, ek_hbm, ev_hbm,
    att, qg, kg, vg, ekg, evg,
    own_ref, slot_ref, q, g, k, v, ek, ev, sem_in,
    send_a, recv_a, send_b, recv_b, tab_a, tab_b, g1, g2, g3, g4,
    pbuf, halo, back_send, back_recv, kacc, vacc, oacc, qacc, kmat, vmat, sel,
    send1, recv1, send2, recv2, send3, recv3, send4, recv4,
    sem_i, sem_h, s1, r1, s2, r2, s3, r3, s4, r4,
):
    me = lax.axis_index("seq")
    t = lax.axis_index("tp")
    x = lax.div(me, 16)
    z = lax.rem(lax.div(me, 4), 4)
    y = lax.rem(me, 4)

    def device(dx, dz, dy, dt):
        return (
            lax.rem(x + dx, 4) * 16 + lax.rem(z + dz, 4) * 4 + lax.rem(y + dy, 4),
            lax.rem(t + dt, 4),
        )

    def seq_peer(d):
        return device(lax.div(d, 16), lax.rem(lax.div(d, 4), 4), lax.rem(d, 4), 0)

    sources = (own_hbm, slot_hbm, k_hbm, v_hbm, q_hbm, g_hbm, ek_hbm, ev_hbm)
    places = (own_ref, slot_ref, k, v, q, g, ek, ev)
    loads = [pltpu.make_async_copy(a, b, sem_in.at[n]) for n, (a, b) in enumerate(zip(sources, places))]
    for load in loads:
        load.start()

    barrier = pltpu.get_barrier_semaphore()

    def greet(d, c):
        pl.semaphore_signal(barrier, 1, device_id=seq_peer(d), device_id_type=MESH)
        return c

    lax.fori_loop(1, 64, greet, 0)
    for dz in range(4):
        for dt in range(1, 4):
            pl.semaphore_signal(barrier, 1, device_id=device(0, dz, 0, dt), device_id_type=MESH)

    loads[0].wait()
    loads[1].wait()

    lane = lax.broadcasted_iota(I32, (1, 128), 1)
    owners = [own_ref[i // 4, i % 4] for i in range(16)]
    slots = [slot_ref[i // 4, i % 4] for i in range(16)]
    row_a = jnp.full((1, 128), -1, I32)
    row_b = jnp.zeros((1, 128), I32)
    row_c = jnp.zeros((1, 128), I32)
    for i in range(16):
        rank = jnp.int32(0)
        for j in range(i):
            rank = rank + (owners[j] == owners[i]).astype(I32)
        place = owners[i] * 2 + rank
        row_a = jnp.where(lane == place, slots[i], row_a)
        row_b = jnp.where(lane == place, i, row_b)
        row_c = jnp.where(lane == i, place, row_c)
        zo = lax.rem(lax.div(owners[i], 4), 4)
        g3[i] = lax.rem(z - zo + 4, 4) * 16 + i
    send_a[0] = row_a
    recv_a[0] = row_a
    rows_bc = jnp.concatenate([row_b, row_c], 0)
    send_b[0] = rows_bc
    recv_b[0] = rows_bc

    def self_block(b, hh):
        cols = pl.ds(pl.multiple_of(hh * 128, 128), 128)
        rows = pl.ds(128 * b, 128)
        if b == 0:
            kk = jnp.concatenate([halo[0, :, cols], k[0:128, cols]], 0)
            vv = jnp.concatenate([halo[1, :, cols], v[0:128, cols]], 0)
        else:
            kk, vv = k[:, cols], v[:, cols]
        heads = [pl.ds(pl.multiple_of(hh * 512 + 128 * u, 128), 128) for u in range(4)]
        qq = jnp.concatenate([q[rows, h] for h in heads], 0)
        gg = jnp.concatenate([g[rows, h] for h in heads], 0)
        r = lax.rem(lax.broadcasted_iota(I32, (512, 256), 0), 128)
        c = lax.broadcasted_iota(I32, (512, 256), 1)
        allowed = (c > r) & (c <= r + 128)
        if b == 0:
            allowed = allowed & (c >= jnp.where(me > 0, 0, 128))
        out, dq, dk, dv = attend(qq, kk, vv, gg, allowed)
        for u in range(4):
            oacc[rows, heads[u]] = out[128 * u : 128 * u + 128]
            qacc[rows, heads[u]] = dq[128 * u : 128 * u + 128]
        if b == 1:
            kacc[:, cols] = dk
            vacc[:, cols] = dv
        else:
            back_send[0, :, cols] = dk[0:128].astype(BF)
            back_send[1, :, cols] = dv[0:128].astype(BF)
            kacc[0:128, cols] = kacc[0:128, cols] + dk[128:256]
            vacc[0:128, cols] = vacc[0:128, cols] + dv[128:256]

    pl.semaphore_wait(barrier, 75)

    nxt = (lax.rem(me + 1, 64), t)
    prv = (lax.rem(me + 63, 64), t)

    def remote(src, dst, ssem, rsem, dev):
        return pltpu.make_async_remote_copy(
            src_ref=src, dst_ref=dst, send_sem=ssem, recv_sem=rsem,
            device_id=dev, device_id_type=MESH,
        )

    def await_bytes(ref, sem):
        pltpu.make_async_copy(ref, ref, sem).wait()

    def tell(d, c):
        remote(send_a.at[0], recv_a.at[d], sem_i.at[0], sem_i.at[1], seq_peer(d)).start()
        return c

    lax.fori_loop(1, 64, tell, 0)
    for dz in range(1, 4):
        remote(send_b.at[0], recv_b.at[dz], sem_i.at[2], sem_i.at[3], device(0, dz, 0, 0)).start()
    for n in range(2, 6):
        loads[n].wait()
    halo_k = remote(k.at[pl.ds(128, 128)], halo.at[0], sem_h.at[0], sem_h.at[1], nxt)
    halo_v = remote(v.at[pl.ds(128, 128)], halo.at[1], sem_h.at[2], sem_h.at[3], nxt)
    halo_k.start()
    halo_v.start()
    self_block(1, 0)
    self_block(1, 1)
    loads[6].wait()
    loads[7].wait()

    await_bytes(recv_a.at[pl.ds(1, 63)], sem_i.at[1])
    await_bytes(recv_b.at[pl.ds(1, 3)], sem_i.at[3])
    copy_a = pltpu.make_async_copy(recv_a, tab_a, sem_i.at[4])
    copy_b = pltpu.make_async_copy(recv_b, tab_b, sem_i.at[5])
    copy_a.start()
    copy_b.start()
    copy_a.wait()
    copy_b.wait()

    def fill1(d, c):
        dx, dy = lax.div(d, 4), lax.rem(d, 4)
        for dz in range(4):
            src = lax.rem(4 - dx, 4) * 16 + ((4 - dz) % 4) * 4 + lax.rem(4 - dy, 4)
            for rank in range(2):
                g1[d * 8 + dz * 2 + rank] = jnp.maximum(tab_a[src, 0, 2 * me + rank], 0)
        return c

    lax.fori_loop(0, 16, fill1, 0)

    def plane_peer(d):
        return device(d // 4, 0, d % 4, 0)

    def stage1(c):
        store = (ek, ev)[c // 4]
        tt = lax.rem(t + c % 4, 4)
        for m in range(8):
            recv1[c][m] = store[g1[m], tt]

        def gather(d, carry):
            for m in range(8):
                send1[c][d * 8 + m] = store[g1[d * 8 + m], tt]
            return carry

        lax.fori_loop(1, 16, gather, 0)

        for d in PLANE:
            part = pl.ds(d * 8, 8)
            remote(send1[c].at[part], recv1[c].at[part], s1.at[c], r1.at[c], plane_peer(d)).start()

    def stage2(c):
        kv, dt = c // 4, c % 4
        low = 1 if dt == 0 else 0
        await_bytes(recv1[c].at[pl.ds(8, 120)], r1.at[c])
        if dt == 0:
            for i in range(16):
                recv2[kv][i] = recv1[c][g2[i]]

        def gather(dz, carry):
            for i in range(16):
                send2[c][dz * 16 + i] = recv1[c][g2[dz * 16 + i]]
            return carry

        lax.fori_loop(low, 4, gather, 0)
        for dz in range(low, 4):
            remote(
                send2[c].at[pl.ds(dz * 16, 16)],
                recv2[kv].at[pl.ds(dt * 64 + dz * 16, 16)],
                s2.at[c], r2.at[c], device(0, dz, 0, dt),
            ).start()

    for c in range(AHEAD):
        stage1(c)

    def fill2(i, c):
        for dz in range(4):
            place = tab_b[(4 - dz) % 4, 1, i]
            owner, rank = lax.div(place, 2), lax.rem(place, 2)
            ox, oy = lax.div(owner, 16), lax.rem(owner, 4)
            dx, dy = lax.rem(x - ox + 4, 4), lax.rem(y - oy + 4, 4)
            g2[dz * 16 + i] = (dx * 4 + dy) * 8 + dz * 2 + rank
        return c

    lax.fori_loop(0, 16, fill2, 0)

    def fill4(d, c):
        dx, dy = lax.div(d, 4), lax.rem(d, 4)
        owner = lax.rem(x + dx, 4) * 16 + z * 4 + lax.rem(y + dy, 4)
        for dz in range(4):
            for rank in range(2):
                g4[d * 8 + dz * 2 + rank] = dz * 16 + tab_b[dz, 0, owner * 2 + rank]
        return c

    lax.fori_loop(0, 16, fill4, 0)

    row_at = lax.broadcasted_iota(I32, (512, 128), 0)
    for w in range(8):
        want = jnp.full((1, 128), -1, I32)
        for n in range(16):
            p = w * 16 + n
            d, dz, rank = p // 8, (p // 2) % 4, p % 2
            got = tab_a[(d // 4) * 16 + dz * 4 + d % 4, 0, 2 * me + rank]
            want = jnp.where(lax.div(lane, 8) == n, got * 8 + lax.rem(lane, 8), want)
        sel[:, pl.ds(128 * w, 128)] = jnp.where(row_at == want, 1.0, 0.0).astype(BF)

    halo_k.wait()
    halo_v.wait()
    self_block(0, 0)
    back_k = remote(back_send.at[0], back_recv.at[0], sem_h.at[4], sem_h.at[5], prv)
    back_v = remote(back_send.at[1], back_recv.at[1], sem_h.at[6], sem_h.at[7], prv)
    def collect(kv):
        for dt in range(4):
            low = 16 if dt == 0 else 0
            await_bytes(recv2[kv].at[pl.ds(dt * 64 + low, 64 - low)], r2.at[kv * 4 + dt])
        mat = (kmat, vmat)[kv]
        for i in range(16):
            for dt in range(4):
                mat[pl.ds(i * 32 + dt * 8, 8), :] = recv2[kv][g3[i] + dt * 64]

    def stretch(ref, cc):
        rows = pl.ds(pl.multiple_of(cc * 64, 64), 64)
        return jnp.concatenate([ref[rows, 128 * h : 128 * h + 128] for h in range(8)], 0)

    def hand_back(kv, cc, grad):
        parts = grad.astype(BF).reshape(16, 8, 128)
        for j in range(4):
            for dt in range(4):
                send3[kv][dt * 16 + cc * 4 + j] = parts[j * 4 + dt]
            recv3[kv * 4][cc * 4 + j] = parts[j * 4]

    def cross_keys(cc, carry):
        near = pl.ds(pl.multiple_of(cc * 128, 128), 128)
        r = lax.broadcasted_iota(I32, (512, 128), 0)
        n = lax.broadcasted_iota(I32, (512, 128), 1)
        allowed = lax.div(r, 256) == lax.div(lax.rem(n, 8), 4)
        p = probs(stretch(q, cc), kmat[near, :], allowed)
        pbuf[cc] = p
        hand_back(1, cc, dot_tn(p.astype(BF), stretch(g, cc)))
        return carry

    def cross_values(cc, carry):
        rows = pl.ds(pl.multiple_of(cc * 64, 64), 64)
        near = pl.ds(pl.multiple_of(cc * 128, 128), 128)
        p = pbuf[cc]
        ds = score_grads(p, vmat[near, :], stretch(g, cc))
        hand_back(0, cc, dot_tn(ds, stretch(q, cc)))
        out = dot_nn(p.astype(BF), vmat[near, :])
        dq = dot_nn(ds, kmat[near, :])
        for h in range(8):
            cols = pl.ds(128 * h, 128)
            att[rows, cols] = (oacc[rows, cols] + out[64 * h : 64 * h + 64]).astype(BF)
            qg[rows, cols] = (qacc[rows, cols] + dq[64 * h : 64 * h + 64]).astype(BF)
        return carry

    def stage3(c):
        kv, dt = c // 4, c % 4
        for dz in range(1 if dt == 0 else 0, 4):
            remote(
                send3[kv].at[pl.ds(dt * 16, 16)],
                recv3[c].at[pl.ds(dz * 16, 16)],
                s3.at[c], r3.at[c], device(0, dz, 0, (4 - dt) % 4),
            ).start()

    def stage4(c):
        low = 16 if c % 4 == 0 else 0
        await_bytes(recv3[c].at[pl.ds(low, 64 - low)], r3.at[c])
        for m in range(8):
            recv4[c][m] = recv3[c][g4[m]]

        def gather(d, carry):
            for m in range(8):
                send4[c][d * 8 + m] = recv3[c][g4[d * 8 + m]]
            return carry

        lax.fori_loop(1, 16, gather, 0)

        for d in PLANE:
            part = pl.ds(d * 8, 8)
            remote(send4[c].at[part], recv4[c].at[part], s4.at[c], r4.at[c], plane_peer(d)).start()

    def gather_store(c):
        await_bytes(recv4[c].at[pl.ds(8, 120)], r4.at[c])
        total = dot_nn(sel[...], recv4[c].reshape(1024, 128)[...])
        (ekg, evg)[c // 4][:, lax.rem(t + c % 4, 4)] = total.reshape(64, 8, 128).astype(BF)

    for c in range(8):
        if c + AHEAD < 8:
            stage1(c + AHEAD)
        stage2(c)
        if c == 1:
            self_block(0, 1)
            back_k.start()
            back_v.start()
        if c == 6:
            collect(0)
            lax.fori_loop(0, 4, cross_keys, 0)

    for c in range(4, 8):
        stage3(c)
    collect(1)
    lax.fori_loop(0, 4, cross_values, 0)
    for c in range(4):
        stage3(c)

    def window_grads():
        back_k.wait()
        back_v.wait()
        kg[0:128, :] = kacc[0:128, :].astype(BF)
        vg[0:128, :] = vacc[0:128, :].astype(BF)
        kg[128:256, :] = (kacc[128:256, :] + back_recv[0].astype(F32)).astype(BF)
        vg[128:256, :] = (vacc[128:256, :] + back_recv[1].astype(F32)).astype(BF)

    order = (4, 5, 6, 7, 0, 1, 2, 3)
    for n in range(8 + LAG):
        if n < 8:
            stage4(order[n])
        if n == 1:
            window_grads()
        if n >= LAG:
            gather_store(order[n - LAG])

    await_bytes(recv_a.at[pl.ds(1, 63)], sem_i.at[0])
    await_bytes(recv_b.at[pl.ds(1, 3)], sem_i.at[2])
    for c in range(8):
        low = 16 if c % 4 == 0 else 0
        await_bytes(send1[c].at[pl.ds(8, 120)], s1.at[c])
        await_bytes(send2[c].at[pl.ds(low, 64 - low)], s2.at[c])
        await_bytes(recv3[c].at[pl.ds(low, 64 - low)], s3.at[c])
        await_bytes(send4[c].at[pl.ds(8, 120)], s4.at[c])


def write_out(*refs):
    copies = [pltpu.make_async_copy(refs[n], refs[6 + n], refs[12].at[n]) for n in range(6)]
    for copy in copies:
        copy.start()
    for copy in copies:
        copy.wait()


def tiles(n):
    return pltpu.VMEM((n, 8, 128), BF)


def body(queries, seq_keys, seq_values, out_grad, enc_keys, enc_values, nbr_owner, nbr_slot):
    def to_tiles(e):
        return e.reshape(64, 4, 4, 2, 128).transpose(0, 2, 3, 1, 4).reshape(64, 4, 8, 128)

    def from_tiles(e):
        return e.reshape(64, 4, 2, 4, 128).transpose(0, 3, 1, 2, 4).reshape(64, 4, 1024)

    hbm = pl.BlockSpec(memory_space=pltpu.HBM)
    vmem = pl.BlockSpec(memory_space=pltpu.VMEM)
    dma = pltpu.SemaphoreType.DMA
    outs = pl.pallas_call(
        kernel,
        out_shape=(
            jax.ShapeDtypeStruct((256, 1024), BF),
            jax.ShapeDtypeStruct((256, 1024), BF),
            jax.ShapeDtypeStruct((256, 256), BF),
            jax.ShapeDtypeStruct((256, 256), BF),
            jax.ShapeDtypeStruct((64, 4, 8, 128), BF),
            jax.ShapeDtypeStruct((64, 4, 8, 128), BF),
        ),
        in_specs=[hbm] * 8,
        out_specs=(vmem,) * 6,
        scratch_shapes=[
            pltpu.SMEM((4, 4), I32),
            pltpu.SMEM((4, 4), I32),
            pltpu.VMEM((256, 1024), BF),
            pltpu.VMEM((256, 1024), BF),
            pltpu.VMEM((256, 256), BF),
            pltpu.VMEM((256, 256), BF),
            pltpu.VMEM((64, 4, 8, 128), BF),
            pltpu.VMEM((64, 4, 8, 128), BF),
            dma((8,)),
            pltpu.VMEM((1, 1, 128), I32),
            pltpu.VMEM((64, 1, 128), I32),
            pltpu.VMEM((1, 2, 128), I32),
            pltpu.VMEM((4, 2, 128), I32),
            pltpu.SMEM((64, 1, 128), I32),
            pltpu.SMEM((4, 2, 128), I32),
            pltpu.SMEM((128,), I32),
            pltpu.SMEM((64,), I32),
            pltpu.SMEM((16,), I32),
            pltpu.SMEM((128,), I32),
            pltpu.VMEM((4, 512, 128), F32),
            pltpu.VMEM((2, 128, 256), BF),
            pltpu.VMEM((2, 128, 256), BF),
            pltpu.VMEM((2, 128, 256), BF),
            pltpu.VMEM((256, 256), F32),
            pltpu.VMEM((256, 256), F32),
            pltpu.VMEM((256, 1024), F32),
            pltpu.VMEM((256, 1024), F32),
            pltpu.VMEM((512, 128), BF),
            pltpu.VMEM((512, 128), BF),
            pltpu.VMEM((512, 1024), BF),
            [tiles(128)] * 8,
            [tiles(128)] * 8,
            [tiles(64)] * 8,
            [tiles(256)] * 2,
            [tiles(64)] * 2,
            [tiles(64)] * 8,
            [tiles(128)] * 8,
            [tiles(128)] * 8,
            dma((6,)),
            dma((8,)),
            dma((8,)),
            dma((8,)),
            dma((8,)),
            dma((8,)),
            dma((8,)),
            dma((8,)),
            dma((8,)),
            dma((8,)),
        ],
        compiler_params=pltpu.CompilerParams(
            collective_id=0, has_side_effects=True, vmem_limit_bytes=VMEM_MAIN
        ),
        name="retro",
    )(
        *[pltpu.with_memory_space_constraint(a, pltpu.HBM) for a in (
            nbr_owner, nbr_slot, queries, out_grad, seq_keys, seq_values,
            to_tiles(enc_keys), to_tiles(enc_values))]
    )
    outs = pl.pallas_call(
        write_out,
        out_shape=tuple(jax.ShapeDtypeStruct(o.shape, BF) for o in outs),
        in_specs=[pl.BlockSpec(memory_space=pl.ANY)] * 6,
        out_specs=(hbm,) * 6,
        scratch_shapes=[dma((6,))],
        compiler_params=pltpu.CompilerParams(vmem_limit_bytes=1 << 20),
        name="write_out",
    )(*outs)
    att, qg, kg, vg, ekg, evg = outs
    return att, qg, kg, vg, from_tiles(ekg), from_tiles(evg)


def solution(mesh):
    shard = P("seq", "tp")
    store = P("seq", "tp", None)
    return jax.shard_map(
        body,
        mesh=mesh,
        in_specs=(shard, shard, shard, shard, store, store, P("seq", None), P("seq", None)),
        out_specs=(shard, shard, shard, shard, store, store),
        check_vma=False,
    )
```
